32 devices in a mesh: groups: 1, ep: 16 (over z, y, x), tp: 2 (over core).
Axes of the slice: x: 2, y: 2, z: 4, core: 2. Of those that a mesh axis runs over, the one named last changes fastest.
Arguments:
- tokens: bfloat16 [1024, 4096], P(('groups', 'ep'), 'tp'), may hold values from -6 to 6
- w_down: bfloat16 [4096, 1024], P('tp', 'ep'), may hold values from -0.09375 to 0.09375
- w_in: bfloat16 [16, 1024, 1344], P('ep', None, 'tp'), may hold values from -0.1875 to 0.1875
- w_out: bfloat16 [16, 1344, 1024], P('ep', 'tp'), may hold values from -0.125 to 0.125
- w_up: bfloat16 [1024, 4096], P('ep', 'tp'), may hold values from -0.1875 to 0.1875
- expert_ids: int32 [1024, 3], P(('groups', 'ep')), may hold values from 0 to 7, all different within a row; in each aligned block of 64 rows (0 to 63, 64 to 127, ...) at most 48 rows name the same one
- route_weights: float32 [1024, 3], P(('groups', 'ep')), may hold values from 0.2 to 1
Outputs:
- layer_out: bfloat16 [1024, 4096], P(('groups', 'ep'), 'tp')
The draws below stay inside these ranges and needn't reach their ends.
Inputs may be any that keep to these rules, and one draw needn't show every extreme that they name: `expert_ids`: each row names 3 different experts. In each aligned block of 64 rows (the rows of one device) no expert is named more than 48 times, a bound that some block reaches.
All inputs are finite; a program needn't handle non-finite values.
Results may differ from the reference program's by a relative error of at most 0.009.
Values may be sent and summed in bfloat16 or wider, within the bound.
A program may use at most 64 MiB of HBM per device.

```python
import math
import jax
import jax.numpy as jnp
import numpy as np
from jax import lax

D = 4096
LATENT = 1024
FF = 2688
TOP = 3
TOK_DEV = 64
EXPERTS = 8
CAP = 48
TOKENS = 1024
N_EP = 16


def block_levels(own_key, dims, pieces, low, high):
    def one(dim, parts):
        draws = jax.random.uniform(jax.random.fold_in(jax.random.fold_in(own_key, 6), dim), (parts,), jnp.float32, low / len(pieces), high / len(pieces))
        return jnp.repeat(jnp.exp(draws), dims[dim] // parts).reshape((-1,) + (1,) * (len(dims) - dim - 1))

    loudness = one(*pieces[0])
    for cut in pieces[1:]:
        loudness = loudness * one(*cut)
    return loudness


def deal_out(stream_key, own, number, rows, amount, top, most, slope):
    ranking = jax.random.permutation(stream_key, amount)
    heavy_load, usual = shares(amount, rows * top, most, slope, True), shares(amount, rows * top, most, slope, False)
    places = jnp.arange(amount)

    def named(lengths, turn):
        used = int((lengths > 0).sum())
        fixed = max(1, used // 4)
        passed = fixed + (places - fixed + turn * (used - fixed)) % max(1, amount - fixed)
        return jnp.zeros((amount,), jnp.int32).at[ranking[jnp.where(places < fixed, places, passed)]].set(jnp.asarray(lengths, jnp.int32))

    lengths = jnp.where(number % 4 == 0, named(heavy_load, number // 4), named(usual, number - number // 4 - 1))
    mixed = jax.random.permutation(jax.random.fold_in(own, 3), amount)
    giver, receiver = mixed[0:amount // 2 * 2:2], mixed[1:amount // 2 * 2:2]
    margin = jnp.minimum(lengths[giver] - 1, most - lengths[receiver]) // 2
    margin = jnp.where((giver == ranking[0]) | (receiver == ranking[0]) | (lengths[receiver] == 0), 0, jnp.maximum(margin, 0))
    passed = jax.random.randint(jax.random.fold_in(own, 4), (amount // 2,), 0, 1 << 20) % (margin + 1)
    lengths = lengths.at[giver].add(-passed).at[receiver].add(passed)
    members = jnp.searchsorted(jnp.cumsum(lengths), jnp.arange(rows * top), side="right").astype(jnp.int32)
    listing = members.reshape(top, rows).T
    listing = listing[jax.random.permutation(jax.random.fold_in(own, 1), rows)]
    turn = jax.random.randint(jax.random.fold_in(own, 2), (rows, 1), 0, top)
    return jnp.take_along_axis(listing, (jnp.arange(top)[None, :] + turn) % top, axis=1)


def shares(count, total, reach, slope, full):
    portions = [(1 << 20) // math.isqrt(grade ** slope) + 1 for grade in range(1, count + 1)]
    largest = reach if full else min(reach, max(-(-total // count), total * portions[0] // sum(portions)))
    least = 1 if total - largest >= count - 1 else 0
    counts, surplus = [largest] + [least] * (count - 1), total - largest - least * (count - 1)
    while surplus > 0:
        movable = [i for i in range(1, count) if counts[i] < largest] or [i for i in range(1, count) if counts[i] < reach]
        mass, left = sum([portions[i] for i in movable]), surplus
        for i in movable:
            more = min(reach - counts[i], max(1, left * portions[i] // mass), surplus)
            counts[i] = counts[i] + more
            surplus = surplus - more
    return np.array(counts)


def normal_values(own_key, shape, deviation, limit, cuts=(), kind=jnp.bfloat16):
    values = jax.random.normal(own_key, shape, jnp.float32) * deviation
    if len(cuts) > 0:
        values = block_levels(own_key, shape, cuts, -0.22, 0.18) * values
    return jnp.clip(values, min=-limit, max=limit).astype(kind)


def setup_inputs(seed: int = 0, part: int = 0) -> dict:
    arg_keys = jax.random.split(jax.random.key(seed), 8)
    own_keys = jax.random.split(jax.random.fold_in(arg_keys[7], part), 8)
    tokens = normal_values(own_keys[0], (TOKENS, D), 1.0, 6.0, ((0, 16), (1, 2)))
    w_down = normal_values(arg_keys[1], (D, LATENT), D ** -0.5, 0.09375, ((0, 2), (1, 16)))
    w_in = normal_values(arg_keys[2], (2 * EXPERTS, LATENT, FF // 2), LATENT ** -0.5, 0.1875, ((0, 16), (2, 2)))
    w_out = normal_values(arg_keys[3], (2 * EXPERTS, FF // 2, LATENT), FF ** -0.5, 0.125, ((0, 16), (1, 2)))
    w_up = normal_values(arg_keys[4], (LATENT, D), LATENT ** -0.5, 0.1875, ((0, 16), (1, 2)))
    expert_ids_keys = jax.random.split(jax.random.fold_in(own_keys[5], 1), TOKENS // TOK_DEV)
    expert_ids_turns = jax.random.permutation(jax.random.fold_in(own_keys[5], 3), TOKENS // TOK_DEV)
    expert_ids = jax.vmap(lambda own, number: deal_out(jax.random.fold_in(own_keys[5], 2), own, number, TOK_DEV, EXPERTS, TOP, CAP, 2))(expert_ids_keys, expert_ids_turns).reshape((TOKENS, TOP))
    route_weights = jnp.clip(0.2 + 0.8 * jax.random.uniform(own_keys[6], (TOKENS, TOP), jnp.float32) ** block_levels(own_keys[6], (TOKENS, TOP), ((0, 16),), -0.2, 0.2), 0.2, 1.0)
    return {"tokens": tokens, "w_down": w_down, "w_in": w_in, "w_out": w_out, "w_up": w_up, "expert_ids": expert_ids, "route_weights": route_weights}


def reference(tokens, w_down, w_in, w_out, w_up, expert_ids, route_weights):
    latent = jnp.dot(tokens, w_down, preferred_element_type=jnp.float32).astype(jnp.bfloat16)
    pairs = TOK_DEV * TOP
    blocks = expert_ids.reshape(N_EP, pairs)
    onehot = (blocks[:, :, None] == jnp.arange(EXPERTS, dtype=jnp.int32)[None, None, :]).astype(jnp.int32)
    before = jnp.cumsum(onehot, axis=1) - onehot
    position = jnp.sum(before * onehot, axis=2).astype(jnp.int32)
    source = jnp.broadcast_to(jnp.arange(N_EP, dtype=jnp.int32)[:, None], (N_EP, pairs))
    owner = source * TOK_DEV + jnp.broadcast_to((jnp.arange(pairs, dtype=jnp.int32) // TOP)[None, :], (N_EP, pairs))
    table = jnp.full((EXPERTS, N_EP, CAP), TOKENS, jnp.int32).at[blocks, source, position].set(owner.astype(jnp.int32))
    weights = jnp.zeros((EXPERTS, N_EP, CAP), jnp.float32).at[blocks, source, position].set(route_weights.reshape(N_EP, pairs).astype(jnp.float32))
    quarter = FF // 4

    def expert_step(total, index):
        rows_of = table[index].reshape(N_EP * CAP)
        slot_weight = weights[index].reshape(N_EP * CAP)
        live = rows_of < TOKENS
        picked = latent[jnp.minimum(rows_of, TOKENS - 1)]
        picked = jnp.where(live[:, None], picked, jnp.zeros_like(picked))
        pair_in = lax.dynamic_slice_in_dim(w_in, (2 * index).astype(jnp.int32), 2, 0)
        pair_out = lax.dynamic_slice_in_dim(w_out, (2 * index).astype(jnp.int32), 2, 0)
        result = jnp.zeros((N_EP * CAP, LATENT), jnp.float32)
        for half in range(2):
            for core in range(2):
                win = pair_in[half][:, core * quarter:(core + 1) * quarter]
                wout = pair_out[half][core * quarter:(core + 1) * quarter, :]
                pre = jnp.maximum(jnp.dot(picked, win, preferred_element_type=jnp.float32), 0.0)
                hidden = (pre * pre).astype(jnp.bfloat16)
                result = result + jnp.dot(hidden, wout, preferred_element_type=jnp.float32)
        total = total.at[rows_of].add(slot_weight[:, None] * result, mode="drop")
        return total, None

    mixed, unused = lax.scan(expert_step, jnp.zeros((TOKENS, LATENT), jnp.float32), jnp.arange(EXPERTS, dtype=jnp.int32))
    mixed = mixed.astype(jnp.bfloat16)
    return jnp.dot(mixed, w_up, preferred_element_type=jnp.float32).astype(jnp.bfloat16)
```

```python
import functools

import jax
import jax.numpy as jnp
from jax import lax
from jax.experimental import pallas as pl
from jax.experimental.pallas import tpu as pltpu
from jax.sharding import PartitionSpec as P

F32 = jnp.float32
BF16 = jnp.bfloat16
LANES = 128


def swapped(value, axis, apart):
    mask = 2**apart
    pairs = [(source, source ^ mask) for source in range(lax.axis_size(axis))]
    return lax.ppermute(value, axis, pairs)


def slot_tables(expert_ids, experts, capacity):
    count, top = expert_ids.shape
    flat = expert_ids.reshape(count * top)
    onehot = (flat[:, None] == jnp.arange(experts, dtype=jnp.int32)[None, :]).astype(jnp.int32)
    before = jnp.cumsum(onehot, axis=0) - onehot
    position = jnp.sum(before * onehot, axis=1)
    place = flat * capacity + position
    sender = jnp.arange(count * top, dtype=jnp.int32) // top
    owner = jnp.full((experts * capacity,), count, jnp.int32).at[place].set(sender)
    return (place, owner)


def per_device(tokens, w_down, w_in, w_out, w_up, expert_ids, route_weights):
    count, top = expert_ids.shape
    devices = lax.axis_size("ep")
    experts = devices // 2
    capacity = 2 * min(count // 2, max(1, count * top // experts))
    halfcap = capacity // 2
    partial_value = jnp.dot(
        tokens, lax.all_gather(w_down, "ep", axis=1, tiled=True), preferred_element_type=jnp.float32
    )
    place, owner = slot_tables(expert_ids, experts, capacity)
    live = owner < count
    source_row = jnp.minimum(owner, count - 1)
    latent = lax.psum(partial_value, "tp").astype(jnp.bfloat16)
    outgoing = latent[source_row]
    outgoing = jnp.where(live[:, None], outgoing, jnp.zeros_like(outgoing))
    outgoing = outgoing.reshape(experts, capacity, outgoing.shape[1])
    outgoing = outgoing.reshape(devices, halfcap, outgoing.shape[2])
    arrived = lax.all_to_all(outgoing, "ep", split_axis=0, concat_axis=0, tiled=True)
    parity = lax.axis_index("ep") % 2
    partner = swapped(arrived, "ep", 0)
    arrived = jnp.where(
        parity == 0,
        jnp.concatenate([arrived, partner], axis=1),
        jnp.concatenate([partner, arrived], axis=1),
    )
    rows = arrived.reshape(devices * capacity, arrived.shape[2])
    pre = jnp.maximum(jnp.dot(rows, w_in[0], preferred_element_type=jnp.float32), 0.0)
    hidden = (pre * pre).astype(jnp.bfloat16)
    result = jnp.dot(hidden, w_out[0], preferred_element_type=jnp.float32)
    result = result.reshape(devices, capacity, result.shape[1])
    width = result.shape[2]
    feature_half = width // 2
    lower = result[:, :, :feature_half]
    upper = result[:, :, feature_half:]
    mine = jnp.where(parity == 0, lower, upper)
    theirs = jnp.where(parity == 0, upper, lower)
    sending = mine + swapped(theirs.astype(jnp.bfloat16), "ep", 0).astype(theirs.dtype)
    returned = lax.all_to_all(sending, "ep", split_axis=0, concat_axis=0, tiled=True)
    summed = returned.reshape(experts, 2, capacity, width // 2)
    summed = jnp.transpose(summed, (0, 2, 1, 3)).reshape(experts * capacity, width)
    picked = summed[place] * route_weights.reshape(count * top)[:, None]
    mixed_part = jnp.sum(picked.reshape(count, top, width), axis=1)
    mixed = lax.psum(mixed_part, "tp").astype(jnp.bfloat16)
    layer_out = jnp.dot(
        mixed, lax.all_gather(w_up, "ep", axis=0, tiled=True), preferred_element_type=jnp.float32
    )
    return layer_out.astype(jnp.bfloat16)


def fused_kernel(
    lines, plane,
    tok_ref, wd_ref, win_hbm, wout_hbm, wup_ref, ids_ref, rw_ref, out_ref,
    tbuf, wbuf, gbuf, ubuf, part, other, latent, win, wout, ykeep, ysend, ycore,
    xsend, yrecv, zsend, zrecv, mbuf, obuf, send_sem, recv_sem, local_sem,
):
    ep = lax.axis_index("ep")
    core = lax.axis_index("tp")
    p = lax.rem(ep, plane)
    z = ep // plane
    mate = 1 - core
    rows, top = ids_ref.shape
    group = lines * rows
    half_rows = group // 2
    cols = wd_ref.shape[0] * plane
    feat = latent.shape[1] // 2
    quarter = ubuf.shape[1]
    ids = iter(range(send_sem.shape[0]))

    def at_plane(j):
        return {"ep": z * plane + (p ^ j), "tp": core}

    def at_line(k):
        return {"ep": (z ^ k) * plane + p, "tp": core}

    at_mate = {"ep": ep, "tp": mate}
    peers = [at_plane(j) for j in range(1, plane)] + [at_line(k) for k in range(1, lines)] + [at_mate]

    def copy(src, dst, device):
        i = next(ids)
        return pltpu.make_async_remote_copy(
            src_ref=src, dst_ref=dst, send_sem=send_sem.at[i], recv_sem=recv_sem.at[i],
            device_id=device, device_id_type=pl.DeviceIdType.MESH,
        )

    started = []

    def start(copies):
        for c in copies:
            c.start()
            started.append(c)
        return copies

    def got(copies):
        for c in copies:
            c.wait_recv()

    def block(index, size):
        return pl.ds(pl.multiple_of(index * size, size), size)

    load_in = pltpu.make_async_copy(win_hbm, win, local_sem.at[0])
    load_out = pltpu.make_async_copy(wout_hbm, wout, local_sem.at[1])
    load_in.start()
    load_out.start()

    barrier = pltpu.get_barrier_semaphore()
    for peer in peers:
        pl.semaphore_signal(barrier, inc=1, device_id=peer, device_id_type=pl.DeviceIdType.MESH)
    lane = lax.broadcasted_iota(jnp.int32, (rows, LANES), 1)
    gates = jnp.zeros((rows, LANES), F32)
    for k in range(top):
        gates += jnp.where(lane == ids_ref[:, k : k + 1], rw_ref[:, k : k + 1], 0.0)
    gbuf[block(p * lines + z, rows), :] = gates
    pl.semaphore_wait(barrier, len(peers))

    t_in = start([copy(tok_ref, tbuf.at[block(z, rows), :], at_line(k)) for k in range(1, lines)])
    w_in_ = start([copy(wd_ref, wbuf.at[block(p, wd_ref.shape[0]), :], at_plane(j)) for j in range(1, plane)])
    g_slice = gbuf.at[block(p * lines + z, rows), :]
    g_line = start([copy(g_slice, g_slice, at_line(k)) for k in range(1, lines)])
    u_slice = ubuf.at[block(ep, rows), :]
    u_plane = start([
        copy(wup_ref.at[:, block(p ^ j, quarter)], u_slice, at_plane(j)) for j in range(1, plane)
    ])
    tbuf[block(z, rows), :] = tok_ref[...]
    wbuf[block(p, wd_ref.shape[0]), :] = wd_ref[...]
    ubuf[block(ep, rows), :] = wup_ref[:, block(p, quarter)]
    got(g_line)
    g_own = gbuf.at[block(p, group), :]
    g_plane = start([copy(g_own, g_own, at_plane(j)) for j in range(1, plane)])
    got(w_in_)
    got(t_in)
    part[...] = lax.dot_general(
        tbuf[...], wbuf[...], (((1,), (1,)), ((), ())), preferred_element_type=F32
    )
    swap = start([copy(part.at[block(mate, half_rows), :], other, at_mate)])
    got(swap)
    own_rows = block(p * 2 + core, half_rows)
    latent[own_rows, block(z, cols)] = (part[block(core, half_rows), :] + other[...]).astype(BF16)
    l_slice = latent.at[own_rows, block(z, cols)]
    l_line = start([copy(l_slice, l_slice, at_line(k)) for k in range(1, lines)])
    got(l_line)
    l_rows = latent.at[own_rows, :]
    l_plane = start([copy(l_rows, l_rows, at_plane(j)) for j in range(1, plane)])
    l_mate = start([copy(l_rows, l_rows, at_mate)])
    got(u_plane)
    u_own = ubuf.at[block(z, plane * rows), :]
    u_line = start([copy(u_own, u_own, at_line(k)) for k in range(1, lines)])
    got(g_plane)
    load_in.wait()
    load_out.wait()

    expert = ep // 2
    glane = lax.broadcasted_iota(jnp.int32, (group, LANES), 1)

    y_core = []
    for j in range(plane):
        if j > 0:
            got([l_plane[j - 1]])
            mine = latent.at[block((p ^ j) * 2 + core, half_rows), :]
            l_mate += start([copy(mine, mine, at_mate)])
        got([l_mate[j]])
        weight = jnp.sum(jnp.where(glane == expert, gbuf[block(p ^ j, group), :], 0.0), axis=1, keepdims=True)
        pre = jnp.dot(latent[block(p ^ j, group), :], win[...], preferred_element_type=F32)
        pre = jnp.maximum(pre, 0.0)
        hidden = (pre * pre).astype(BF16)
        ysend[j] = (
            weight * jnp.dot(hidden, wout[:, block(mate, feat)], preferred_element_type=F32)
        ).astype(BF16)
        y_core += start([copy(ysend.at[j], ycore.at[j], at_mate)])
        ykeep[j] = weight * jnp.dot(hidden, wout[:, block(core, feat)], preferred_element_type=F32)
    y_plane = []
    for j in range(1, plane):
        got([y_core[j]])
        xsend[j] = (ykeep[j] + ycore[j].astype(F32)).astype(BF16)
        y_plane += start([copy(xsend.at[j], yrecv.at[j], at_plane(j))])
    got([y_core[0]])
    total = ykeep[0] + ycore[0].astype(F32)
    for j in range(1, plane):
        got([y_plane[j - 1]])
        total += yrecv[j].astype(F32)
    ykeep[0] = total
    zsend[...] = total.astype(BF16)
    z_line = start([
        copy(zsend.at[block(z ^ k, rows), :], zrecv.at[k], at_line(k)) for k in range(1, lines)
    ])
    got(z_line)
    mixed = ykeep[0, block(z, rows), :]
    for k in range(1, lines):
        mixed += zrecv[k].astype(F32)
    mbuf[block(p, rows), block(core, feat)] = mixed.astype(BF16)
    m_own = mbuf.at[block(p, rows), block(core, feat)]
    m_plane = start([copy(m_own, m_own, at_plane(j)) for j in range(1, plane)])
    m_mate = start([copy(m_own, m_own, at_mate)])
    for j in range(1, plane):
        got([m_plane[j - 1]])
        m_slice = mbuf.at[block(p ^ j, rows), block(core, feat)]
        m_mate += start([copy(m_slice, m_slice, at_mate)])
    got(u_line)
    got(m_mate)
    obuf[...] = jnp.dot(mbuf[...], ubuf[...], preferred_element_type=F32).astype(BF16)
    o_plane = start([
        copy(obuf.at[block(p ^ j, rows), :], out_ref.at[:, block(p, quarter)], at_plane(j))
        for j in range(1, plane)
    ])
    out_ref[:, block(p, quarter)] = obuf[block(p, rows), :]
    got(o_plane)
    for c in started:
        c.wait_send()


def fused(tokens, w_down, w_in, w_out, w_up, expert_ids, route_weights, lines, plane):
    count, model = tokens.shape
    width = w_in.shape[1]
    hidden = w_in.shape[2]
    group = count * lines
    everyone = group * plane
    feat = width // 2
    quarter = w_up.shape[1] // plane
    copies = 6 * (lines - 1) + 6 * (plane - 1) + 2 + (plane - 1) * 2 + plane * 2 + 8
    vmem = pl.BlockSpec(memory_space=pltpu.VMEM)
    hbm = pl.BlockSpec(memory_space=pl.ANY)
    return pl.pallas_call(
        functools.partial(fused_kernel, lines, plane),
        out_shape=jax.ShapeDtypeStruct((count, w_up.shape[1]), BF16),
        in_specs=[vmem, vmem, hbm, hbm, vmem, vmem, vmem],
        out_specs=vmem,
        scratch_shapes=[
            pltpu.VMEM((group, model), BF16),
            pltpu.VMEM((w_down.shape[1] * plane, model), BF16),
            pltpu.VMEM((everyone, LANES), F32),
            pltpu.VMEM((width, quarter), BF16),
            pltpu.VMEM((group, w_down.shape[1] * plane), F32),
            pltpu.VMEM((group // 2, w_down.shape[1] * plane), F32),
            pltpu.VMEM((everyone, width), BF16),
            pltpu.VMEM((width, hidden), BF16),
            pltpu.VMEM((hidden, width), BF16),
            pltpu.VMEM((plane, group, feat), F32),
            pltpu.VMEM((plane, group, feat), BF16),
            pltpu.VMEM((plane, group, feat), BF16),
            pltpu.VMEM((plane, group, feat), BF16),
            pltpu.VMEM((plane, group, feat), BF16),
            pltpu.VMEM((group, feat), BF16),
            pltpu.VMEM((lines, count, feat), BF16),
            pltpu.VMEM((plane * count, width), BF16),
            pltpu.VMEM((plane * count, quarter), BF16),
            pltpu.SemaphoreType.DMA((copies,)),
            pltpu.SemaphoreType.DMA((copies,)),
            pltpu.SemaphoreType.DMA((2,)),
        ],
        compiler_params=pltpu.CompilerParams(
            collective_id=0, has_side_effects=True, vmem_limit_bytes=60 * 2**20
        ),
    )(tokens, w_down.T, w_in[0], w_out[0], w_up, expert_ids, route_weights)


def grid_of(devices):
    bits = devices.bit_length() - 1
    plane = 2 ** ((bits + 1) // 2)
    return devices // plane, plane


def solution(mesh):
    in_specs = (
        P(("groups", "ep"), "tp"),
        P("tp", "ep"),
        P("ep", None, "tp"),
        P("ep", "tp", None),
        P("ep", "tp"),
        P(("groups", "ep"), None),
        P(("groups", "ep"), None),
    )
    out_specs = P(("groups", "ep"), "tp")
    devices = mesh.shape["ep"]
    lines, plane = grid_of(devices)

    def body(tokens, w_down, w_in, w_out, w_up, expert_ids, route_weights):
        args = (tokens, w_down, w_in, w_out, w_up, expert_ids, route_weights)
        everyone = tokens.shape[0] * devices
        resident = everyone * w_in.shape[1] * 10
        if resident <= 2**24 and lines * plane == devices and mesh.shape["tp"] == 2:
            return fused(*args, lines, plane)
        return per_device(*args)

    return jax.shard_map(body, mesh=mesh, in_specs=in_specs, out_specs=out_specs, check_vma=False)
```

```python
import jax
import jax.numpy as jnp
from jax import lax
from jax.experimental import pallas as pl
from jax.experimental.pallas import tpu as pltpu
from jax.sharding import PartitionSpec as P

F32 = jnp.float32
BF16 = jnp.bfloat16
LINKS = 2**4
CHUNKS = 4
COPIES = 128


def swapped(value, axis, apart):
    mask = 2**apart
    pairs = [(source, source ^ mask) for source in range(lax.axis_size(axis))]
    return lax.ppermute(value, axis, pairs)


def slot_tables(expert_ids, experts, capacity):
    count, top = expert_ids.shape
    flat = expert_ids.reshape(count * top)
    onehot = (flat[:, None] == jnp.arange(experts, dtype=jnp.int32)[None, :]).astype(jnp.int32)
    before = jnp.cumsum(onehot, axis=0) - onehot
    position = jnp.sum(before * onehot, axis=1)
    place = flat * capacity + position
    sender = jnp.arange(count * top, dtype=jnp.int32) // top
    owner = jnp.full((experts * capacity,), count, jnp.int32).at[place].set(sender)
    return (place, owner)


def per_device(tokens, w_down, w_in, w_out, w_up, expert_ids, route_weights):
    count, top = expert_ids.shape
    devices = lax.axis_size("ep")
    experts = devices // 2
    capacity = 2 * min(count // 2, max(1, count * top // experts))
    halfcap = capacity // 2
    partial_value = jnp.dot(
        tokens, lax.all_gather(w_down, "ep", axis=1, tiled=True), preferred_element_type=jnp.float32
    )
    place, owner = slot_tables(expert_ids, experts, capacity)
    live = owner < count
    source_row = jnp.minimum(owner, count - 1)
    latent = lax.psum(partial_value, "tp").astype(jnp.bfloat16)
    outgoing = latent[source_row]
    outgoing = jnp.where(live[:, None], outgoing, jnp.zeros_like(outgoing))
    outgoing = outgoing.reshape(experts, capacity, outgoing.shape[1])
    outgoing = outgoing.reshape(devices, halfcap, outgoing.shape[2])
    arrived = lax.all_to_all(outgoing, "ep", split_axis=0, concat_axis=0, tiled=True)
    parity = lax.axis_index("ep") % 2
    partner = swapped(arrived, "ep", 0)
    arrived = jnp.where(
        parity == 0,
        jnp.concatenate([arrived, partner], axis=1),
        jnp.concatenate([partner, arrived], axis=1),
    )
    rows = arrived.reshape(devices * capacity, arrived.shape[2])
    pre = jnp.maximum(jnp.dot(rows, w_in[0], preferred_element_type=jnp.float32), 0.0)
    hidden = (pre * pre).astype(jnp.bfloat16)
    result = jnp.dot(hidden, w_out[0], preferred_element_type=jnp.float32)
    result = result.reshape(devices, capacity, result.shape[1])
    width = result.shape[2]
    feature_half = width // 2
    lower = result[:, :, :feature_half]
    upper = result[:, :, feature_half:]
    mine = jnp.where(parity == 0, lower, upper)
    theirs = jnp.where(parity == 0, upper, lower)
    sending = mine + swapped(theirs.astype(jnp.bfloat16), "ep", 0).astype(theirs.dtype)
    returned = lax.all_to_all(sending, "ep", split_axis=0, concat_axis=0, tiled=True)
    summed = returned.reshape(experts, 2, capacity, width // 2)
    summed = jnp.transpose(summed, (0, 2, 1, 3)).reshape(experts * capacity, width)
    picked = summed[place] * route_weights.reshape(count * top)[:, None]
    mixed_part = jnp.sum(picked.reshape(count, top, width), axis=1)
    mixed = lax.psum(mixed_part, "tp").astype(jnp.bfloat16)
    layer_out = jnp.dot(
        mixed, lax.all_gather(w_up, "ep", axis=0, tiled=True), preferred_element_type=jnp.float32
    )
    return layer_out.astype(jnp.bfloat16)


def fused_kernel(
    tok_ref, wd_ref, win_hbm, wout_hbm, wup_ref, ids_ref, rw_ref, out_ref,
    tbuf, wbuf, gbuf, ubuf, part, other, latent, win, wout, ykeep, ysend, ycore,
    xsend, yrecv, zsend, zrecv, mbuf, obuf, send_sem, recv_sem, local_sem,
):
    ep = lax.axis_index("ep")
    core = lax.axis_index("tp")
    p = lax.rem(ep, 4)
    z = ep // 4
    x = lax.rem(ep, 2)
    y = lax.rem(ep // 2, 2)
    z0 = lax.rem(ep // 4, 2)
    z1 = ep // 8
    mate = 1 - core
    top, rows = ids_ref.shape
    model = tok_ref.shape[1]
    group = 4 * rows
    cols = wd_ref.shape[0]
    feat = latent.shape[1] // 2
    quarter = ubuf.shape[1]
    experts = gbuf.shape[0] // LINKS
    ids = iter(range(send_sem.shape[0]))

    def at(mask):
        return {"ep": ep ^ mask, "tp": core}

    at_mate = {"ep": ep, "tp": mate}
    peers = [at(mask) for mask in (1, 2, 3, 4, 8, 12)] + [at_mate]
    started = []

    def send(src, dst, device):
        i = next(ids)
        c = pltpu.make_async_remote_copy(
            src_ref=src, dst_ref=dst, send_sem=send_sem.at[i], recv_sem=recv_sem.at[i],
            device_id=device, device_id_type=pl.DeviceIdType.MESH,
        )
        c.start()
        started.append(c)
        return c

    def got(*copies):
        for c in copies:
            c.wait_recv()

    def block(index, size):
        return pl.ds(pl.multiple_of(index * size, size), size)

    barrier = pltpu.get_barrier_semaphore()
    for peer in peers:
        pl.semaphore_signal(barrier, inc=1, device_id=peer, device_id_type=pl.DeviceIdType.MESH)
    pair = 2 * cols
    loads = [pltpu.make_async_copy(wout_hbm, wout, local_sem.at[8])]
    for n in range(8):
        a, b, c = n // 4, n // 2 % 2, n % 2
        loads.append(pltpu.make_async_copy(
            win_hbm.at[:, pl.ds((a * 4 + b * 2 + c) * pair, pair)],
            win.at[:, pl.ds((c * 4 + b * 2 + a) * pair, pair)],
            local_sem.at[n],
        ))
    for load in loads:
        load.start()
    lane = lax.broadcasted_iota(jnp.int32, (experts, rows), 0)
    gates = jnp.zeros((experts, rows), F32)
    for k in range(top):
        gates += jnp.where(lane == ids_ref[k : k + 1, :], rw_ref[k : k + 1, :], 0.0)
    gbuf[block(p * 4 + z, experts), :] = gates
    pl.semaphore_wait(barrier, len(peers))

    step = model // CHUNKS
    t_slot, w_slot = block(y * 2 + z0, rows), block(z1 * 2 + x, cols)
    t_far, w_far = [], []
    for n in range(CHUNKS):
        part_n = pl.ds(n * step, step)
        t_far.append(send(tok_ref.at[:, part_n], tbuf.at[t_slot, part_n], at(4)))
        w_far.append(send(wd_ref.at[:, part_n], wbuf.at[w_slot, part_n], at(8)))
    arrivals = [send(tok_ref, tbuf.at[t_slot, :], at(2)), send(wd_ref, wbuf.at[w_slot, :], at(1))]
    tbuf[t_slot, :] = tok_ref[...]
    wbuf[w_slot, :] = wd_ref[...]
    ubuf[block(ep, rows), :] = wup_ref[:, block(p, quarter)]
    g_slice = gbuf.at[block(p * 4 + z, experts), :]
    g_line = [send(g_slice, g_slice, at(4 * k)) for k in (1, 2, 3)]
    for n in range(CHUNKS):
        part_n = pl.ds(n * step, step)
        got(t_far[n])
        t_next = tbuf.at[block(y * 2 + (1 - z0), rows), part_n]
        arrivals.append(send(t_next, t_next, at(2)))
        got(w_far[n])
        w_next = wbuf.at[block((1 - z1) * 2 + x, cols), part_n]
        arrivals.append(send(w_next, w_next, at(1)))
    got(*g_line)
    g_own = gbuf.at[block(p, 4 * experts), :]
    g_plane = [send(g_own, g_own, at(j)) for j in (1, 2, 3)]
    got(*arrivals)
    part[...] = lax.dot_general(
        tbuf[...], wbuf[...], (((1,), (1,)), ((), ())), preferred_element_type=F32
    )
    got(send(part.at[block(mate, 2 * rows), :], other, at_mate))

    def piece(xx, zz1, yy, zz0):
        return latent.at[block((core * 2 + xx) * 2 + zz1, 2 * rows), block(yy * 2 + zz0, 4 * cols)]

    own = piece(x, z1, y, z0)
    own[...] = (part[block(core, 2 * rows), :] + other[...]).astype(BF16)
    l_line = {k: send(own, own, at(4 * k)) for k in (1, 2, 3)}
    l_plane = {}
    for k in range(4):
        if k > 0:
            got(l_line[k])
        src = piece(x, z1 ^ (k // 2), y, z0 ^ (k % 2))
        for j in (2, 1, 3):
            l_plane[j, k] = send(src, src, at(j))
    u_slice = ubuf.at[block(ep, rows), :]
    u_plane = [send(wup_ref.at[:, block(p ^ j, quarter)], u_slice, at(j)) for j in (1, 2, 3)]

    def to_mate(xx, columns):
        src = latent.at[block(core * 2 + xx, group), columns]
        return send(src, src, at_mate)

    got(*[l_plane[2, k] for k in range(4)])
    near = to_mate(x, pl.ds(0, 2 * feat))
    got(*[l_plane[1, k] for k in range(4)])
    far = [to_mate(1 - x, block(y, feat))]
    got(*u_plane)
    u_own = ubuf.at[block(z, 4 * rows), :]
    u_line = [send(u_own, u_own, at(4 * k)) for k in (1, 2, 3)]
    got(*g_plane)
    for load in loads:
        load.wait()
    gate_rows = gbuf[...].T
    glane = lax.broadcasted_iota(jnp.int32, gate_rows.shape, 1)
    expert = ep // 2
    y_core, y_plane = {}, {}

    def compute(j):
        gi = p ^ j
        weight = jnp.concatenate([
            jnp.sum(jnp.where(glane == (gi * 4 + k) * experts + expert, gate_rows, 0.0), axis=1, keepdims=True)
            for k in range(4)
        ], axis=0)
        pre = lax.dot_general(
            latent[block(gi, group), :], win[...], (((1,), (1,)), ((), ())), preferred_element_type=F32
        )
        pre = jnp.maximum(pre, 0.0)
        hidden = (pre * pre).astype(BF16)
        ysend[j] = (
            weight * jnp.dot(hidden, wout[:, block(mate, feat)], preferred_element_type=F32)
        ).astype(BF16)
        y_core[j] = send(ysend.at[j], ycore.at[j], at_mate)
        ykeep[j] = weight * jnp.dot(hidden, wout[:, block(core, feat)], preferred_element_type=F32)

    def drain(j):
        got(y_core[j])
        xsend[j] = (ykeep[j] + ycore[j].astype(F32)).astype(BF16)
        for k in (3, 2, 1, 0):
            r = block(z ^ k, rows)
            y_plane[j, k] = send(xsend.at[j, r, :], yrecv.at[j, r, :], at(j))

    got(near)
    compute(2)
    compute(0)
    drain(2)
    got(*[l_plane[3, k] for k in range(4)])
    far.append(to_mate(1 - x, block(1 - y, feat)))
    got(*far)
    compute(3)
    compute(1)
    drain(3)
    drain(1)
    got(y_core[0])
    z_line = {}
    for k in (3, 2, 1, 0):
        r = block(z ^ k, rows)
        total = ykeep[0, r, :] + ycore[0, r, :].astype(F32)
        for j in (2, 3, 1):
            got(y_plane[j, k])
            total += yrecv[j, r, :].astype(F32)
        if k > 0:
            zsend[k] = total.astype(BF16)
            z_line[k] = send(zsend.at[k], zrecv.at[k], at(4 * k))
        else:
            mixed = total
    for k in (1, 2, 3):
        got(z_line[k])
        mixed += zrecv[k].astype(F32)
    mbuf[block(p, rows), block(core, feat)] = mixed.astype(BF16)
    m_own = mbuf.at[block(p, rows), block(core, feat)]
    m_plane = [send(m_own, m_own, at(j)) for j in (1, 2, 3)]
    m_mate = [send(m_own, m_own, at_mate)]
    for j in (1, 2, 3):
        got(m_plane[j - 1])
        m_slice = mbuf.at[block(p ^ j, rows), block(core, feat)]
        m_mate.append(send(m_slice, m_slice, at_mate))
    got(*u_line)
    got(*m_mate)
    obuf[...] = jnp.dot(mbuf[...], ubuf[...], preferred_element_type=F32).astype(BF16)
    o_plane = [
        send(obuf.at[block(p ^ j, rows), :], out_ref.at[:, block(p, quarter)], at(j)) for j in (1, 2, 3)
    ]
    out_ref[:, block(p, quarter)] = obuf[block(p, rows), :]
    got(*o_plane)
    for c in started:
        c.wait_send()


def fused(tokens, w_down, w_in, w_out, w_up, expert_ids, route_weights):
    count, model = tokens.shape
    width = w_in.shape[1]
    hidden = w_in.shape[2]
    group = 4 * count
    cols = 4 * w_down.shape[1]
    feat = width // 2
    quarter = w_up.shape[1] // 4
    vmem = pl.BlockSpec(memory_space=pltpu.VMEM)
    hbm = pl.BlockSpec(memory_space=pl.ANY)
    return pl.pallas_call(
        fused_kernel,
        out_shape=jax.ShapeDtypeStruct((count, w_up.shape[1]), BF16),
        in_specs=[vmem, vmem, hbm, hbm, vmem, vmem, vmem],
        out_specs=vmem,
        scratch_shapes=[
            pltpu.VMEM((group, model), BF16),
            pltpu.VMEM((cols, model), BF16),
            pltpu.VMEM((LINKS * (LINKS // 2), count), F32),
            pltpu.VMEM((width, quarter), BF16),
            pltpu.VMEM((group, cols), F32),
            pltpu.VMEM((group // 2, cols), F32),
            pltpu.VMEM((LINKS * count, width), BF16),
            pltpu.VMEM((hidden, width), BF16),
            pltpu.VMEM((hidden, width), BF16),
            pltpu.VMEM((4, group, feat), F32),
            pltpu.VMEM((4, group, feat), BF16),
            pltpu.VMEM((4, group, feat), BF16),
            pltpu.VMEM((4, group, feat), BF16),
            pltpu.VMEM((4, group, feat), BF16),
            pltpu.VMEM((4, count, feat), BF16),
            pltpu.VMEM((4, count, feat), BF16),
            pltpu.VMEM((group, width), BF16),
            pltpu.VMEM((group, quarter), BF16),
            pltpu.SemaphoreType.DMA((COPIES,)),
            pltpu.SemaphoreType.DMA((COPIES,)),
            pltpu.SemaphoreType.DMA((9,)),
        ],
        compiler_params=pltpu.CompilerParams(
            collective_id=0, has_side_effects=True, vmem_limit_bytes=60 * 2**20
        ),
    )(tokens, w_down.T, w_in[0].T, w_out[0], w_up, expert_ids.T, route_weights.T)


def solution(mesh):
    in_specs = (
        P(("groups", "ep"), "tp"),
        P("tp", "ep"),
        P("ep", None, "tp"),
        P("ep", "tp", None),
        P("ep", "tp"),
        P(("groups", "ep"), None),
        P(("groups", "ep"), None),
    )
    out_specs = P(("groups", "ep"), "tp")
    devices = mesh.shape["ep"]

    def body(tokens, w_down, w_in, w_out, w_up, expert_ids, route_weights):
        args = (tokens, w_down, w_in, w_out, w_up, expert_ids, route_weights)
        everyone = tokens.shape[0] * devices
        resident = everyone * w_in.shape[1] * 10
        if resident <= 2**24 and devices == LINKS and mesh.shape["tp"] == 2:
            return fused(*args)
        return per_device(*args)

    return jax.shard_map(body, mesh=mesh, in_specs=in_specs, out_specs=out_specs, check_vma=False)
```

```python
import jax
import jax.numpy as jnp
from jax import lax
from jax.experimental import pallas as pl
from jax.experimental.pallas import tpu as pltpu
from jax.sharding import PartitionSpec as P

F32 = jnp.float32
BF16 = jnp.bfloat16
LINKS = 2**4
CHUNKS = 4
COPIES = 128


def swapped(value, axis, apart):
    mask = 2**apart
    pairs = [(source, source ^ mask) for source in range(lax.axis_size(axis))]
    return lax.ppermute(value, axis, pairs)


def slot_tables(expert_ids, experts, capacity):
    count, top = expert_ids.shape
    flat = expert_ids.reshape(count * top)
    onehot = (flat[:, None] == jnp.arange(experts, dtype=jnp.int32)[None, :]).astype(jnp.int32)
    before = jnp.cumsum(onehot, axis=0) - onehot
    position = jnp.sum(before * onehot, axis=1)
    place = flat * capacity + position
    sender = jnp.arange(count * top, dtype=jnp.int32) // top
    owner = jnp.full((experts * capacity,), count, jnp.int32).at[place].set(sender)
    return (place, owner)


def per_device(tokens, w_down, w_in, w_out, w_up, expert_ids, route_weights):
    count, top = expert_ids.shape
    devices = lax.axis_size("ep")
    experts = devices // 2
    capacity = 2 * min(count // 2, max(1, count * top // experts))
    halfcap = capacity // 2
    partial_value = jnp.dot(
        tokens, lax.all_gather(w_down, "ep", axis=1, tiled=True), preferred_element_type=jnp.float32
    )
    place, owner = slot_tables(expert_ids, experts, capacity)
    live = owner < count
    source_row = jnp.minimum(owner, count - 1)
    latent = lax.psum(partial_value, "tp").astype(jnp.bfloat16)
    outgoing = latent[source_row]
    outgoing = jnp.where(live[:, None], outgoing, jnp.zeros_like(outgoing))
    outgoing = outgoing.reshape(experts, capacity, outgoing.shape[1])
    outgoing = outgoing.reshape(devices, halfcap, outgoing.shape[2])
    arrived = lax.all_to_all(outgoing, "ep", split_axis=0, concat_axis=0, tiled=True)
    parity = lax.axis_index("ep") % 2
    partner = swapped(arrived, "ep", 0)
    arrived = jnp.where(
        parity == 0,
        jnp.concatenate([arrived, partner], axis=1),
        jnp.concatenate([partner, arrived], axis=1),
    )
    rows = arrived.reshape(devices * capacity, arrived.shape[2])
    pre = jnp.maximum(jnp.dot(rows, w_in[0], preferred_element_type=jnp.float32), 0.0)
    hidden = (pre * pre).astype(jnp.bfloat16)
    result = jnp.dot(hidden, w_out[0], preferred_element_type=jnp.float32)
    result = result.reshape(devices, capacity, result.shape[1])
    width = result.shape[2]
    feature_half = width // 2
    lower = result[:, :, :feature_half]
    upper = result[:, :, feature_half:]
    mine = jnp.where(parity == 0, lower, upper)
    theirs = jnp.where(parity == 0, upper, lower)
    sending = mine + swapped(theirs.astype(jnp.bfloat16), "ep", 0).astype(theirs.dtype)
    returned = lax.all_to_all(sending, "ep", split_axis=0, concat_axis=0, tiled=True)
    summed = returned.reshape(experts, 2, capacity, width // 2)
    summed = jnp.transpose(summed, (0, 2, 1, 3)).reshape(experts * capacity, width)
    picked = summed[place] * route_weights.reshape(count * top)[:, None]
    mixed_part = jnp.sum(picked.reshape(count, top, width), axis=1)
    mixed = lax.psum(mixed_part, "tp").astype(jnp.bfloat16)
    layer_out = jnp.dot(
        mixed, lax.all_gather(w_up, "ep", axis=0, tiled=True), preferred_element_type=jnp.float32
    )
    return layer_out.astype(jnp.bfloat16)


def fused_kernel(
    tok_ref, wd_ref, win_hbm, wout_hbm, wup_ref, ids_ref, rw_ref, out_ref,
    tbuf, wbuf, gbuf, ubuf, part, other, latent, win, wout, ykeep, ysend, ycore,
    xsend, yrecv, zsend, zrecv, mbuf, obuf, send_sem, recv_sem, local_sem,
):
    ep = lax.axis_index("ep")
    core = lax.axis_index("tp")
    p = lax.rem(ep, 4)
    z = ep // 4
    x = lax.rem(ep, 2)
    y = lax.rem(ep // 2, 2)
    z0 = lax.rem(ep // 4, 2)
    z1 = ep // 8
    mate = 1 - core
    top, rows = ids_ref.shape
    model = tok_ref.shape[1]
    group = 4 * rows
    cols = wd_ref.shape[0]
    feat = latent.shape[1] // 2
    quarter = ubuf.shape[1]
    experts = gbuf.shape[0] // LINKS
    ids = iter(range(send_sem.shape[0]))

    def at(mask):
        return {"ep": ep ^ mask, "tp": core}

    at_mate = {"ep": ep, "tp": mate}
    peers = [at(mask) for mask in (1, 2, 3, 4, 8, 12)] + [at_mate]
    started = []

    def send(src, dst, device):
        i = next(ids)
        c = pltpu.make_async_remote_copy(
            src_ref=src, dst_ref=dst, send_sem=send_sem.at[i], recv_sem=recv_sem.at[i],
            device_id=device, device_id_type=pl.DeviceIdType.MESH,
        )
        c.start()
        started.append(c)
        return c

    def got(*copies):
        for c in copies:
            c.wait_recv()

    def block(index, size):
        return pl.ds(pl.multiple_of(index * size, size), size)

    barrier = pltpu.get_barrier_semaphore()
    for peer in peers:
        pl.semaphore_signal(barrier, inc=1, device_id=peer, device_id_type=pl.DeviceIdType.MESH)
    pair = 2 * cols
    loads = [pltpu.make_async_copy(wout_hbm, wout, local_sem.at[8])]
    for n in range(8):
        a, b, c = n // 4, n // 2 % 2, n % 2
        loads.append(pltpu.make_async_copy(
            win_hbm.at[:, pl.ds((a * 4 + b * 2 + c) * pair, pair)],
            win.at[:, pl.ds((c * 4 + b * 2 + a) * pair, pair)],
            local_sem.at[n],
        ))
    for load in loads:
        load.start()
    lane = lax.broadcasted_iota(jnp.int32, (experts, rows), 0)
    gates = jnp.zeros((experts, rows), F32)
    for k in range(top):
        gates += jnp.where(lane == ids_ref[k : k + 1, :], rw_ref[k : k + 1, :], 0.0)
    gbuf[block(p * 4 + z, experts), :] = gates
    pl.semaphore_wait(barrier, len(peers))

    step = model // CHUNKS
    t_slot, w_slot = block(y * 2 + z0, rows), block(z1 * 2 + x, cols)
    t_far, w_far = [], []
    for n in range(CHUNKS):
        part_n = pl.ds(n * step, step)
        t_far.append(send(tok_ref.at[:, part_n], tbuf.at[t_slot, part_n], at(4)))
        w_far.append(send(wd_ref.at[:, part_n], wbuf.at[w_slot, part_n], at(8)))
    arrivals = [send(tok_ref, tbuf.at[t_slot, :], at(2)), send(wd_ref, wbuf.at[w_slot, :], at(1))]
    tbuf[t_slot, :] = tok_ref[...]
    wbuf[w_slot, :] = wd_ref[...]
    ubuf[block(ep, rows), :] = wup_ref[:, block(p, quarter)]
    g_slice = gbuf.at[block(p * 4 + z, experts), :]
    g_line = [send(g_slice, g_slice, at(4 * k)) for k in (1, 2, 3)]
    for n in range(CHUNKS):
        part_n = pl.ds(n * step, step)
        got(t_far[n])
        t_next = tbuf.at[block(y * 2 + (1 - z0), rows), part_n]
        arrivals.append(send(t_next, t_next, at(2)))
        got(w_far[n])
        w_next = wbuf.at[block((1 - z1) * 2 + x, cols), part_n]
        arrivals.append(send(w_next, w_next, at(1)))
    got(*g_line)
    g_own = gbuf.at[block(p, 4 * experts), :]
    g_plane = [send(g_own, g_own, at(j)) for j in (1, 2, 3)]
    u_slice = ubuf.at[block(ep, rows), :]
    u_plane = [send(wup_ref.at[:, block(p ^ j, quarter)], u_slice, at(j)) for j in (1, 2, 3)]
    got(*arrivals)
    part[...] = lax.dot_general(
        tbuf[...], wbuf[...], (((1,), (1,)), ((), ())), preferred_element_type=F32
    )
    got(send(part.at[block(mate, 2 * rows), :], other, at_mate))

    def piece(xx, zz1, yy, zz0):
        return latent.at[block((core * 2 + xx) * 2 + zz1, 2 * rows), block(yy * 2 + zz0, 4 * cols)]

    own = piece(x, z1, y, z0)
    own[...] = (part[block(core, 2 * rows), :] + other[...]).astype(BF16)
    l_line = {k: send(own, own, at(4 * k)) for k in (1, 2, 3)}
    got(*u_plane)
    u_own = ubuf.at[block(z, 4 * rows), :]
    u_line = [send(u_own, u_own, at(4 * k)) for k in (1, 2, 3)]
    side, ahead = 1 + core, 2 - core
    l_side, l_ahead, l_diag = [], [], []
    for k in range(4):
        if k > 0:
            got(l_line[k])
        src = piece(x, z1 ^ (k // 2), y, z0 ^ (k % 2))
        l_side.append(send(src, src, at(side)))
        l_ahead.append(send(src, src, at(ahead)))
    for k in range(4):
        got(l_side[k])
        src = piece(x ^ (1 - core), z1 ^ (k // 2), y ^ core, z0 ^ (k % 2))
        l_diag.append(send(src, src, at(ahead)))
    def to_mate(xx, columns):
        src = latent.at[block(core * 2 + xx, group), columns]
        return send(src, src, at_mate)

    got(*l_ahead)
    near = to_mate(x, pl.ds(0, 2 * feat))
    far = [to_mate(1 - x, block(y, feat))]
    got(*g_plane)
    for load in loads:
        load.wait()
    gate_rows = gbuf[...].T
    glane = lax.broadcasted_iota(jnp.int32, gate_rows.shape, 1)
    expert = ep // 2
    y_core, y_plane = {}, {}

    def compute(j):
        gi = p ^ j
        weight = jnp.concatenate([
            jnp.sum(jnp.where(glane == (gi * 4 + k) * experts + expert, gate_rows, 0.0), axis=1, keepdims=True)
            for k in range(4)
        ], axis=0)
        pre = lax.dot_general(
            latent[block(gi, group), :], win[...], (((1,), (1,)), ((), ())), preferred_element_type=F32
        )
        pre = jnp.maximum(pre, 0.0)
        hidden = (pre * pre).astype(BF16)
        ysend[j] = (
            weight * jnp.dot(hidden, wout[:, block(mate, feat)], preferred_element_type=F32)
        ).astype(BF16)
        y_core[j] = send(ysend.at[j], ycore.at[j], at_mate)
        ykeep[j] = weight * jnp.dot(hidden, wout[:, block(core, feat)], preferred_element_type=F32)

    def drain(j):
        got(y_core[j])
        xsend[j] = (ykeep[j] + ycore[j].astype(F32)).astype(BF16)
        for k in (3, 2, 1, 0):
            r = block(z ^ k, rows)
            y_plane[j, k] = send(xsend.at[j, r, :], yrecv.at[j, r, :], at(j))

    got(near)
    compute(2)
    compute(0)
    drain(2)
    got(*l_diag)
    far.append(to_mate(1 - x, block(1 - y, feat)))
    got(*far)
    compute(3)
    compute(1)
    drain(3)
    drain(1)
    got(y_core[0])
    z_line = {}
    for k in (3, 2, 1, 0):
        r = block(z ^ k, rows)
        total = ykeep[0, r, :] + ycore[0, r, :].astype(F32)
        for j in (2, 3, 1):
            got(y_plane[j, k])
            total += yrecv[j, r, :].astype(F32)
        if k > 0:
            zsend[k] = total.astype(BF16)
            z_line[k] = send(zsend.at[k], zrecv.at[k], at(4 * k))
        else:
            mixed = total
    for k in (1, 2, 3):
        got(z_line[k])
        mixed += zrecv[k].astype(F32)
    mbuf[block(p, rows), block(core, feat)] = mixed.astype(BF16)
    m_own = mbuf.at[block(p, rows), block(core, feat)]
    m_plane = [send(m_own, m_own, at(j)) for j in (1, 2, 3)]
    m_mate = [send(m_own, m_own, at_mate)]
    for j in (1, 2, 3):
        got(m_plane[j - 1])
        m_slice = mbuf.at[block(p ^ j, rows), block(core, feat)]
        m_mate.append(send(m_slice, m_slice, at_mate))
    got(*u_line)
    got(*m_mate)
    obuf[...] = jnp.dot(mbuf[...], ubuf[...], preferred_element_type=F32).astype(BF16)
    o_plane = [
        send(obuf.at[block(p ^ j, rows), :], out_ref.at[:, block(p, quarter)], at(j)) for j in (1, 2, 3)
    ]
    out_ref[:, block(p, quarter)] = obuf[block(p, rows), :]
    got(*o_plane)
    for c in started:
        c.wait_send()


def fused(tokens, w_down, w_in, w_out, w_up, expert_ids, route_weights):
    count, model = tokens.shape
    width = w_in.shape[1]
    hidden = w_in.shape[2]
    group = 4 * count
    cols = 4 * w_down.shape[1]
    feat = width // 2
    quarter = w_up.shape[1] // 4
    vmem = pl.BlockSpec(memory_space=pltpu.VMEM)
    hbm = pl.BlockSpec(memory_space=pl.ANY)
    return pl.pallas_call(
        fused_kernel,
        out_shape=jax.ShapeDtypeStruct((count, w_up.shape[1]), BF16),
        in_specs=[vmem, vmem, hbm, hbm, vmem, vmem, vmem],
        out_specs=vmem,
        scratch_shapes=[
            pltpu.VMEM((group, model), BF16),
            pltpu.VMEM((cols, model), BF16),
            pltpu.VMEM((LINKS * (LINKS // 2), count), F32),
            pltpu.VMEM((width, quarter), BF16),
            pltpu.VMEM((group, cols), F32),
            pltpu.VMEM((group // 2, cols), F32),
            pltpu.VMEM((LINKS * count, width), BF16),
            pltpu.VMEM((hidden, width), BF16),
            pltpu.VMEM((hidden, width), BF16),
            pltpu.VMEM((4, group, feat), F32),
            pltpu.VMEM((4, group, feat), BF16),
            pltpu.VMEM((4, group, feat), BF16),
            pltpu.VMEM((4, group, feat), BF16),
            pltpu.VMEM((4, group, feat), BF16),
            pltpu.VMEM((4, count, feat), BF16),
            pltpu.VMEM((4, count, feat), BF16),
            pltpu.VMEM((group, width), BF16),
            pltpu.VMEM((group, quarter), BF16),
            pltpu.SemaphoreType.DMA((COPIES,)),
            pltpu.SemaphoreType.DMA((COPIES,)),
            pltpu.SemaphoreType.DMA((9,)),
        ],
        compiler_params=pltpu.CompilerParams(
            collective_id=0, has_side_effects=True, vmem_limit_bytes=60 * 2**20
        ),
    )(tokens, w_down.T, w_in[0].T, w_out[0], w_up, expert_ids.T, route_weights.T)


def solution(mesh):
    in_specs = (
        P(("groups", "ep"), "tp"),
        P("tp", "ep"),
        P("ep", None, "tp"),
        P("ep", "tp", None),
        P("ep", "tp"),
        P(("groups", "ep"), None),
        P(("groups", "ep"), None),
    )
    out_specs = P(("groups", "ep"), "tp")
    devices = mesh.shape["ep"]

    def body(tokens, w_down, w_in, w_out, w_up, expert_ids, route_weights):
        args = (tokens, w_down, w_in, w_out, w_up, expert_ids, route_weights)
        everyone = tokens.shape[0] * devices
        resident = everyone * w_in.shape[1] * 10
        if resident <= 2**24 and devices == LINKS and mesh.shape["tp"] == 2:
            return fused(*args)
        return per_device(*args)

    return jax.shard_map(body, mesh=mesh, in_specs=in_specs, out_specs=out_specs, check_vma=False)
```

```python
import jax
import jax.numpy as jnp
from jax import lax
from jax.experimental import pallas as pl
from jax.experimental.pallas import tpu as pltpu
from jax.sharding import PartitionSpec as P

F32 = jnp.float32
BF16 = jnp.bfloat16
LINKS = 2**4
CHUNKS = 8
COPIES = 128


def swapped(value, axis, apart):
    mask = 2**apart
    pairs = [(source, source ^ mask) for source in range(lax.axis_size(axis))]
    return lax.ppermute(value, axis, pairs)


def slot_tables(expert_ids, experts, capacity):
    count, top = expert_ids.shape
    flat = expert_ids.reshape(count * top)
    onehot = (flat[:, None] == jnp.arange(experts, dtype=jnp.int32)[None, :]).astype(jnp.int32)
    before = jnp.cumsum(onehot, axis=0) - onehot
    position = jnp.sum(before * onehot, axis=1)
    place = flat * capacity + position
    sender = jnp.arange(count * top, dtype=jnp.int32) // top
    owner = jnp.full((experts * capacity,), count, jnp.int32).at[place].set(sender)
    return (place, owner)


def per_device(tokens, w_down, w_in, w_out, w_up, expert_ids, route_weights):
    count, top = expert_ids.shape
    devices = lax.axis_size("ep")
    experts = devices // 2
    capacity = 2 * min(count // 2, max(1, count * top // experts))
    halfcap = capacity // 2
    partial_value = jnp.dot(
        tokens, lax.all_gather(w_down, "ep", axis=1, tiled=True), preferred_element_type=jnp.float32
    )
    place, owner = slot_tables(expert_ids, experts, capacity)
    live = owner < count
    source_row = jnp.minimum(owner, count - 1)
    latent = lax.psum(partial_value, "tp").astype(jnp.bfloat16)
    outgoing = latent[source_row]
    outgoing = jnp.where(live[:, None], outgoing, jnp.zeros_like(outgoing))
    outgoing = outgoing.reshape(experts, capacity, outgoing.shape[1])
    outgoing = outgoing.reshape(devices, halfcap, outgoing.shape[2])
    arrived = lax.all_to_all(outgoing, "ep", split_axis=0, concat_axis=0, tiled=True)
    parity = lax.axis_index("ep") % 2
    partner = swapped(arrived, "ep", 0)
    arrived = jnp.where(
        parity == 0,
        jnp.concatenate([arrived, partner], axis=1),
        jnp.concatenate([partner, arrived], axis=1),
    )
    rows = arrived.reshape(devices * capacity, arrived.shape[2])
    pre = jnp.maximum(jnp.dot(rows, w_in[0], preferred_element_type=jnp.float32), 0.0)
    hidden = (pre * pre).astype(jnp.bfloat16)
    result = jnp.dot(hidden, w_out[0], preferred_element_type=jnp.float32)
    result = result.reshape(devices, capacity, result.shape[1])
    width = result.shape[2]
    feature_half = width // 2
    lower = result[:, :, :feature_half]
    upper = result[:, :, feature_half:]
    mine = jnp.where(parity == 0, lower, upper)
    theirs = jnp.where(parity == 0, upper, lower)
    sending = mine + swapped(theirs.astype(jnp.bfloat16), "ep", 0).astype(theirs.dtype)
    returned = lax.all_to_all(sending, "ep", split_axis=0, concat_axis=0, tiled=True)
    summed = returned.reshape(experts, 2, capacity, width // 2)
    summed = jnp.transpose(summed, (0, 2, 1, 3)).reshape(experts * capacity, width)
    picked = summed[place] * route_weights.reshape(count * top)[:, None]
    mixed_part = jnp.sum(picked.reshape(count, top, width), axis=1)
    mixed = lax.psum(mixed_part, "tp").astype(jnp.bfloat16)
    layer_out = jnp.dot(
        mixed, lax.all_gather(w_up, "ep", axis=0, tiled=True), preferred_element_type=jnp.float32
    )
    return layer_out.astype(jnp.bfloat16)


def fused_kernel(
    tok_ref, wd_ref, win_hbm, wout_hbm, wup_ref, ids_ref, rw_ref, out_ref,
    tbuf, wbuf, gbuf, ubuf, part, other, latent, win, wout, ykeep, ysend, ycore,
    xsend, yrecv, zsend, zrecv, mbuf, obuf, send_sem, recv_sem, local_sem,
):
    ep = lax.axis_index("ep")
    core = lax.axis_index("tp")
    p = lax.rem(ep, 4)
    z = ep // 4
    x = lax.rem(ep, 2)
    y = lax.rem(ep // 2, 2)
    z0 = lax.rem(ep // 4, 2)
    z1 = ep // 8
    mate = 1 - core
    top, rows = ids_ref.shape
    model = tok_ref.shape[1]
    group = 4 * rows
    cols = wd_ref.shape[0]
    feat = latent.shape[1] // 2
    quarter = ubuf.shape[1]
    experts = gbuf.shape[0] // LINKS
    ids = iter(range(send_sem.shape[0]))

    def at(mask):
        return {"ep": ep ^ mask, "tp": core}

    at_mate = {"ep": ep, "tp": mate}
    peers = [at(mask) for mask in (1, 2, 3, 4, 8, 12)] + [at_mate]
    started = []

    def send(src, dst, device):
        i = next(ids)
        c = pltpu.make_async_remote_copy(
            src_ref=src, dst_ref=dst, send_sem=send_sem.at[i], recv_sem=recv_sem.at[i],
            device_id=device, device_id_type=pl.DeviceIdType.MESH,
        )
        c.start()
        started.append(c)
        return c

    def got(*copies):
        for c in copies:
            c.wait_recv()

    def block(index, size):
        return pl.ds(pl.multiple_of(index * size, size), size)

    barrier = pltpu.get_barrier_semaphore()
    for peer in peers:
        pl.semaphore_signal(barrier, inc=1, device_id=peer, device_id_type=pl.DeviceIdType.MESH)
    pair = 2 * cols
    loads = [pltpu.make_async_copy(wout_hbm, wout, local_sem.at[8])]
    for n in range(8):
        a, b, c = n // 4, n // 2 % 2, n % 2
        loads.append(pltpu.make_async_copy(
            win_hbm.at[:, pl.ds((a * 4 + b * 2 + c) * pair, pair)],
            win.at[:, pl.ds((c * 4 + b * 2 + a) * pair, pair)],
            local_sem.at[n],
        ))
    for load in loads:
        load.start()
    lane = lax.broadcasted_iota(jnp.int32, (experts, rows), 0)
    gates = jnp.zeros((experts, rows), F32)
    for k in range(top):
        gates += jnp.where(lane == ids_ref[k : k + 1, :], rw_ref[k : k + 1, :], 0.0)
    gbuf[block(p * 4 + z, experts), :] = gates
    pl.semaphore_wait(barrier, len(peers))

    step = model // CHUNKS
    t_slot, w_slot = block(y * 2 + z0, rows), block(z1 * 2 + x, cols)
    t_far, w_far = [], []
    for n in range(CHUNKS):
        part_n = pl.ds(n * step, step)
        t_far.append(send(tok_ref.at[:, part_n], tbuf.at[t_slot, part_n], at(4)))
        w_far.append(send(wd_ref.at[:, part_n], wbuf.at[w_slot, part_n], at(8)))
    arrivals = [send(tok_ref, tbuf.at[t_slot, :], at(2)), send(wd_ref, wbuf.at[w_slot, :], at(1))]
    tbuf[t_slot, :] = tok_ref[...]
    wbuf[w_slot, :] = wd_ref[...]
    ubuf[block(ep, rows), :] = wup_ref[:, block(p, quarter)]
    g_slice = gbuf.at[block(p * 4 + z, experts), :]
    g_line = [send(g_slice, g_slice, at(4 * k)) for k in (1, 2, 3)]
    for n in range(CHUNKS):
        part_n = pl.ds(n * step, step)
        got(t_far[n])
        t_next = tbuf.at[block(y * 2 + (1 - z0), rows), part_n]
        arrivals.append(send(t_next, t_next, at(2)))
        got(w_far[n])
        w_next = wbuf.at[block((1 - z1) * 2 + x, cols), part_n]
        arrivals.append(send(w_next, w_next, at(1)))
    got(*g_line)
    g_own = gbuf.at[block(p, 4 * experts), :]
    g_plane = [send(g_own, g_own, at(j)) for j in (1, 2, 3)]
    u_slice = ubuf.at[block(ep, rows), :]
    u_plane = [send(wup_ref.at[:, block(p ^ j, quarter)], u_slice, at(j)) for j in (1, 2, 3)]
    got(*arrivals)
    part[...] = lax.dot_general(
        tbuf[...], wbuf[...], (((1,), (1,)), ((), ())), preferred_element_type=F32
    )
    got(send(part.at[block(mate, 2 * rows), :], other, at_mate))

    def piece(xx, zz1, yy, zz0):
        return latent.at[block((core * 2 + xx) * 2 + zz1, 2 * rows), block(yy * 2 + zz0, 4 * cols)]

    own = piece(x, z1, y, z0)
    own[...] = (part[block(core, 2 * rows), :] + other[...]).astype(BF16)
    l_line = {k: send(own, own, at(4 * k)) for k in (1, 2, 3)}
    got(*u_plane)
    u_own = ubuf.at[block(z, 4 * rows), :]
    u_line = [send(u_own, u_own, at(4 * k)) for k in (1, 2, 3)]
    side, ahead = 1 + core, 2 - core
    l_side, l_ahead, l_diag = [], [], []
    for k in range(4):
        if k > 0:
            got(l_line[k])
        src = piece(x, z1 ^ (k // 2), y, z0 ^ (k % 2))
        l_side.append(send(src, src, at(side)))
        l_ahead.append(send(src, src, at(ahead)))
    for k in range(4):
        got(l_side[k])
        src = piece(x ^ (1 - core), z1 ^ (k // 2), y ^ core, z0 ^ (k % 2))
        l_diag.append(send(src, src, at(ahead)))
    def to_mate(xx, columns):
        src = latent.at[block(core * 2 + xx, group), columns]
        return send(src, src, at_mate)

    got(*l_ahead)
    near = to_mate(x, pl.ds(0, 2 * feat))
    far = [to_mate(1 - x, block(y, feat))]
    got(*g_plane)
    for load in loads:
        load.wait()
    gate_rows = gbuf[...].T
    glane = lax.broadcasted_iota(jnp.int32, gate_rows.shape, 1)
    expert = ep // 2
    y_core, y_plane = {}, {}

    def compute(j):
        gi = p ^ j
        weight = jnp.concatenate([
            jnp.sum(jnp.where(glane == (gi * 4 + k) * experts + expert, gate_rows, 0.0), axis=1, keepdims=True)
            for k in range(4)
        ], axis=0)
        pre = lax.dot_general(
            latent[block(gi, group), :], win[...], (((1,), (1,)), ((), ())), preferred_element_type=F32
        )
        pre = jnp.maximum(pre, 0.0)
        hidden = (pre * pre).astype(BF16)
        ysend[j] = (
            weight * jnp.dot(hidden, wout[:, block(mate, feat)], preferred_element_type=F32)
        ).astype(BF16)
        y_core[j] = send(ysend.at[j], ycore.at[j], at_mate)
        ykeep[j] = weight * jnp.dot(hidden, wout[:, block(core, feat)], preferred_element_type=F32)

    def drain(j):
        got(y_core[j])
        xsend[j] = (ykeep[j] + ycore[j].astype(F32)).astype(BF16)
        for k in (3, 2, 1, 0):
            r = block(z ^ k, rows)
            y_plane[j, k] = send(xsend.at[j, r, :], yrecv.at[j, r, :], at(j))

    got(*l_diag)
    far.append(to_mate(1 - x, block(1 - y, feat)))
    got(near, *far)
    compute(3)
    compute(1)
    drain(3)
    compute(2)
    drain(1)
    compute(0)
    drain(2)
    got(y_core[0])
    z_line = {}
    for k in (3, 2, 1, 0):
        r = block(z ^ k, rows)
        total = ykeep[0, r, :] + ycore[0, r, :].astype(F32)
        for j in (3, 1, 2):
            got(y_plane[j, k])
            total += yrecv[j, r, :].astype(F32)
        if k > 0:
            zsend[k] = total.astype(BF16)
            z_line[k] = send(zsend.at[k], zrecv.at[k], at(4 * k))
        else:
            mixed = total
    for k in (1, 2, 3):
        got(z_line[k])
        mixed += zrecv[k].astype(F32)
    mbuf[block(p, rows), block(core, feat)] = mixed.astype(BF16)
    m_own = mbuf.at[block(p, rows), block(core, feat)]
    m_plane = [send(m_own, m_own, at(j)) for j in (1, 2, 3)]
    m_mate = [send(m_own, m_own, at_mate)]
    for j in (1, 2, 3):
        got(m_plane[j - 1])
        m_slice = mbuf.at[block(p ^ j, rows), block(core, feat)]
        m_mate.append(send(m_slice, m_slice, at_mate))
    got(*u_line)
    got(*m_mate)
    obuf[...] = jnp.dot(mbuf[...], ubuf[...], preferred_element_type=F32).astype(BF16)
    o_plane = [
        send(obuf.at[block(p ^ j, rows), :], out_ref.at[:, block(p, quarter)], at(j)) for j in (1, 2, 3)
    ]
    out_ref[:, block(p, quarter)] = obuf[block(p, rows), :]
    got(*o_plane)
    for c in started:
        c.wait_send()


def fused(tokens, w_down, w_in, w_out, w_up, expert_ids, route_weights):
    count, model = tokens.shape
    width = w_in.shape[1]
    hidden = w_in.shape[2]
    group = 4 * count
    cols = 4 * w_down.shape[1]
    feat = width // 2
    quarter = w_up.shape[1] // 4
    vmem = pl.BlockSpec(memory_space=pltpu.VMEM)
    hbm = pl.BlockSpec(memory_space=pl.ANY)
    return pl.pallas_call(
        fused_kernel,
        out_shape=jax.ShapeDtypeStruct((count, w_up.shape[1]), BF16),
        in_specs=[vmem, vmem, hbm, hbm, vmem, vmem, vmem],
        out_specs=vmem,
        scratch_shapes=[
            pltpu.VMEM((group, model), BF16),
            pltpu.VMEM((cols, model), BF16),
            pltpu.VMEM((LINKS * (LINKS // 2), count), F32),
            pltpu.VMEM((width, quarter), BF16),
            pltpu.VMEM((group, cols), F32),
            pltpu.VMEM((group // 2, cols), F32),
            pltpu.VMEM((LINKS * count, width), BF16),
            pltpu.VMEM((hidden, width), BF16),
            pltpu.VMEM((hidden, width), BF16),
            pltpu.VMEM((4, group, feat), F32),
            pltpu.VMEM((4, group, feat), BF16),
            pltpu.VMEM((4, group, feat), BF16),
            pltpu.VMEM((4, group, feat), BF16),
            pltpu.VMEM((4, group, feat), BF16),
            pltpu.VMEM((4, count, feat), BF16),
            pltpu.VMEM((4, count, feat), BF16),
            pltpu.VMEM((group, width), BF16),
            pltpu.VMEM((group, quarter), BF16),
            pltpu.SemaphoreType.DMA((COPIES,)),
            pltpu.SemaphoreType.DMA((COPIES,)),
            pltpu.SemaphoreType.DMA((9,)),
        ],
        compiler_params=pltpu.CompilerParams(
            collective_id=0, has_side_effects=True, vmem_limit_bytes=60 * 2**20
        ),
    )(tokens, w_down.T, w_in[0].T, w_out[0], w_up, expert_ids.T, route_weights.T)


def solution(mesh):
    in_specs = (
        P(("groups", "ep"), "tp"),
        P("tp", "ep"),
        P("ep", None, "tp"),
        P("ep", "tp", None),
        P("ep", "tp"),
        P(("groups", "ep"), None),
        P(("groups", "ep"), None),
    )
    out_specs = P(("groups", "ep"), "tp")
    devices = mesh.shape["ep"]

    def body(tokens, w_down, w_in, w_out, w_up, expert_ids, route_weights):
        args = (tokens, w_down, w_in, w_out, w_up, expert_ids, route_weights)
        everyone = tokens.shape[0] * devices
        resident = everyone * w_in.shape[1] * 10
        if resident <= 2**24 and devices == LINKS and mesh.shape["tp"] == 2:
            return fused(*args)
        return per_device(*args)

    return jax.shard_map(body, mesh=mesh, in_specs=in_specs, out_specs=out_specs, check_vma=False)
```
